32 devices in a mesh: row: 4 (over x, core), col: 8 (over z, y).
Axes of the slice: x: 2, y: 2, z: 4, core: 2. Of those that a mesh axis runs over, the one named last changes fastest.
Arguments:
- old_table: float32 [8, 4096, 128], P('col', 'row'), may hold values from -1 to 1
- old_blocks: int32 [8, 32], P('col', 'row'), may hold values from 0 to 31, as said below
- new_blocks: int32 [8, 32], P('col', 'row'), may hold values from 0 to 31, as said below
- bag_row_index: int32 [512, 8, 64], P(None, 'col'), may hold values from 0 to 4095
- bag_length: int32 [512, 8], P(None, 'col'), may hold values from 1 to 64
- dense: bfloat16 [512, 128], P(('row', 'col')), may hold values from -6 to 6
- w_first: bfloat16 [164, 1024], replicated, may hold values from -1 to 1
- w_second: bfloat16 [1024, 1024], replicated, may hold values from -0.25 to 0.25
- w_out: bfloat16 [1024], replicated, may hold values from -0.75 to 0.75
Outputs:
- logits: float32 [512], P(('row', 'col'))
- new_tables: float32 [8, 4096, 128], P('col', 'row')
The draws below stay inside these ranges and needn't reach their ends.
Inputs may be any that keep to these rules, and one draw needn't show every extreme that they name: `old_blocks`: for each table a permutation of the blocks; row device r holds positions r * 8 to (r + 1) * 8 - 1. For each table a permutation of the blocks; for every ordered pair of row devices, exactly 2 of the blocks that the first holds in old_blocks lie on the second in new_blocks.
All inputs are finite; a program needn't handle non-finite values.
Results may differ from the reference program's by a relative error of at most 0.0069.
Values sent between devices are 32-bit elements; how exact they have to be, the bound alone decides.
A program may use at most 64 MiB of HBM per device.

```python
import math
import jax
import jax.numpy as jnp
import numpy as np
from jax import lax

EMBED_WIDTH = 128
H = 1024
BLK = 128
L = 64
SLOTS = 8
NTAB = 8
NBLK = 32
MOVE = 2
TROWS = 4096
SAMPLES = 512
F = 164
N_ROW = 4


def layout_pair(key):
    table_keys = jax.random.split(jax.random.fold_in(key, 7), NTAB)

    def one_table(table_key):
        first_key, second_key, third_key = jax.random.split(table_key, 3)
        before = jax.random.permutation(first_key, NBLK).astype(jnp.int32)
        shuffled = jax.vmap(lambda inner: jax.random.permutation(inner, SLOTS))(jax.random.split(second_key, N_ROW))
        anchor = jnp.arange(N_ROW, dtype=jnp.int32)[:, None] * SLOTS + shuffled.astype(jnp.int32)
        offered = anchor.reshape(N_ROW, N_ROW, MOVE).transpose(1, 0, 2).reshape(N_ROW, SLOTS)
        placing = jax.vmap(lambda inner: jax.random.permutation(inner, SLOTS))(jax.random.split(third_key, N_ROW))
        taken = jnp.take_along_axis(offered, placing.astype(jnp.int32), axis=1).reshape(NBLK)
        after = jnp.take(before, taken, axis=0)
        return (before, after)
    return jax.vmap(one_table)(table_keys)


def draw_old_blocks(key, part):
    return layout_pair(key)[0]


def draw_new_blocks(key, part):
    return layout_pair(key)[1]


def set_ends(array, stream_key, least, top_value):
    longest = array.shape.index(max(array.shape))
    spots = []
    for shift in (0, 1):
        where = [jax.random.randint(jax.random.fold_in(stream_key, axis), (), 0, length) for axis, length in enumerate(array.shape)]
        where[longest] = (where[longest] + shift) % array.shape[longest]
        spots.append(tuple(where))
    return array.at[spots[0]].set(least).at[spots[1]].set(top_value)


def shard_levels(own_key, extent, pieces, least, top_value):
    loudness = 1.0
    for axis_at, parts in pieces:
        steps = jax.random.uniform(jax.random.fold_in(jax.random.fold_in(own_key, 6), axis_at), (parts,), jnp.float32, least / len(pieces), top_value / len(pieces))
        loudness = loudness * jnp.repeat(jnp.exp(steps), extent[axis_at] // parts).reshape((-1,) + (1,) * (len(extent) - 1 - axis_at))
    return loudness


def cumulative_ranks(amount, lean):
    loads = [(1 << 20) // math.isqrt(rank ** lean) + 1 for rank in range(1, amount + 1)]
    deviation = 1 + sum(loads) // (1 << 30)
    return np.cumsum(np.array([max(1, weight // deviation) for weight in loads]))


def ranked_ids(rng, extent, amount, slope):
    grid = cumulative_ranks(amount, slope)
    lot = jax.random.randint(jax.random.fold_in(rng, 1), extent, 0, int(grid[amount - 1]))
    grade = jnp.searchsorted(jnp.asarray(grid, jnp.int32), lot, side="right")
    return jax.random.permutation(jax.random.fold_in(rng, 2), amount)[grade].astype(jnp.int32)


def scatter_about(key, extent, width, reach, cuts=(), held_as=jnp.bfloat16):
    entries = jax.random.normal(key, extent, jnp.float32) * width
    if len(cuts) > 0:
        entries = shard_levels(key, extent, cuts, -0.22, 0.18) * entries
    return jnp.clip(entries, min=-reach, max=reach).astype(held_as)


def setup_inputs(seed: int = 0) -> dict:
    arg_keys = jax.random.split(jax.random.key(seed), 10)
    return {
        "old_table": scatter_about(arg_keys[0], (NTAB, TROWS, EMBED_WIDTH), 0.125, 1.0, ((0, 8), (1, 4)), jnp.float32),
        "old_blocks": draw_old_blocks(jax.random.fold_in(arg_keys[9], 71), 0),
        "new_blocks": draw_new_blocks(jax.random.fold_in(arg_keys[9], 71), 0),
        "bag_row_index": set_ends(ranked_ids(arg_keys[3], (SAMPLES, NTAB, L), TROWS, 2), jax.random.fold_in(arg_keys[3], 3), 0, TROWS - 1).astype(jnp.int32),
        "bag_length": set_ends(jax.random.randint(arg_keys[4], (SAMPLES, NTAB), 1, L + 1), jax.random.fold_in(arg_keys[4], 1), 1, L).astype(jnp.int32),
        "dense": scatter_about(arg_keys[5], (SAMPLES, EMBED_WIDTH), 1.0, 6.0, ((0, 32),)),
        "w_first": scatter_about(arg_keys[6], (F, H), (F // 4) ** -0.5, 1.0),
        "w_second": scatter_about(arg_keys[7], (H, H), (H // 2) ** -0.5, 0.25),
        "w_out": scatter_about(arg_keys[8], (H,), (H // 16) ** -0.5, 0.75),
    }


strict_precision = lax.Precision.HIGHEST


def pool_table(operands):
    table_rows, indices, weights = operands
    return jnp.sum(jnp.take(table_rows, indices, axis=0) * weights[:, :, None], axis=1)


def reference(old_table, old_blocks, new_blocks, bag_row_index, bag_length, dense, w_first, w_second, w_out):
    stored = old_table.reshape(NTAB, NBLK, BLK, EMBED_WIDTH)
    tables = jnp.arange(NTAB, dtype=jnp.int32)[:, None]
    logical = jnp.zeros_like(stored).at[tables, old_blocks.astype(jnp.int32)].set(stored)
    new_tables = logical[tables, new_blocks.astype(jnp.int32)].reshape(NTAB, TROWS, EMBED_WIDTH)
    is_live = (jnp.arange(L, dtype=jnp.int32)[None, None, :] < bag_length[:, :, None]).astype(jnp.float32)
    pooled = lax.map(pool_table, (logical.reshape(NTAB, TROWS, EMBED_WIDTH), jnp.transpose(bag_row_index, (1, 0, 2)), jnp.transpose(is_live, (1, 0, 2))))
    pooled = jnp.transpose(pooled, (1, 0, 2))
    dense_wide = dense.astype(jnp.float32)
    stacked_vectors = jnp.concatenate([dense_wide[:, None, :], pooled], axis=1)
    interaction_matrix = jnp.einsum("cxp,cfp->cxf", stacked_vectors, stacked_vectors, precision=strict_precision) * (EMBED_WIDTH ** -0.5)
    upper_index, lower_index = np.triu_indices(NTAB + 1, 1)
    crossed = interaction_matrix[:, upper_index, lower_index]
    joined = jnp.concatenate([dense_wide, crossed], axis=1).astype(jnp.bfloat16)
    hidden_one = jnp.maximum(jnp.dot(joined, w_first, preferred_element_type=jnp.float32), 0.0).astype(jnp.bfloat16)
    hidden_two = jnp.maximum(jnp.dot(hidden_one, w_second, preferred_element_type=jnp.float32), 0.0).astype(jnp.bfloat16)
    logits = jnp.dot(hidden_two, w_out, preferred_element_type=jnp.float32)
    return logits, new_tables
```

```python
import functools

import jax
import jax.numpy as jnp
import numpy as np
from jax import lax
from jax.experimental import pallas as pl
from jax.experimental.pallas import tpu as pltpu
from jax.sharding import PartitionSpec as P

MESH = pl.DeviceIdType.MESH
LANES = 128
FAR = 1 << 20


def row_peer(r, q, n, sign):
    chips = n // 2
    return lax.rem(r // 2 + (sign * (q // 2)) % chips, chips) * 2 + lax.rem(r % 2 + q % 2, 2)


def far_first(n):
    return sorted(range(1, n), key=lambda q: -(q // 2))


def everywhere(reduce, x):
    return reduce(reduce(x, axis=1, keepdims=True), axis=0, keepdims=True)


def least(x):
    return everywhere(jnp.min, x)


def choose(which, reads):
    first = reads[0]()
    rows, width = first.shape
    wide = jnp.broadcast_to(which, (8, width))
    picked = first.reshape(rows // 8, 8, width)
    for at, read in enumerate(reads[1:], 1):
        picked = jnp.where((wide == at)[None], read().reshape(rows // 8, 8, width), picked)
    return picked.reshape(rows, width)


def kernel(
    n_row, n_col,
    old_ref, new_ref, table_hbm, idx_hbm, len_hbm,
    out_ref, pooled_ref,
    table_ref, idx_ref, len_ref, ids, ids_in, blocks_out, blocks_in, halves, counts,
    part, part_in, total, swap_in,
    load_sem, ids_sem, ids_rsem, blk_sem, blk_rsem, part_sem, part_rsem, swap_sem, swap_rsem,
):
    r, c = lax.axis_index("row"), lax.axis_index("col")
    slots = old_ref.shape[1]
    blk = table_ref.shape[0] // slots
    width = table_ref.shape[1]
    move = slots // n_row
    samples, bag = idx_ref.shape
    share = samples // n_row
    each = share // n_col
    pack = LANES // bag
    group = 8 * pack
    tile = min(share, 128)

    loads = [
        pltpu.make_async_copy(idx_hbm, idx_ref, load_sem.at[0]),
        pltpu.make_async_copy(len_hbm, len_ref, load_sem.at[1]),
        pltpu.make_async_copy(table_hbm, table_ref, load_sem.at[2]),
    ]
    for load in loads:
        load.start()

    barrier = pltpu.get_barrier_semaphore()
    for q in range(1, n_row):
        pl.semaphore_signal(barrier, inc=1, device_id={"row": row_peer(r, q, n_row, 1)}, device_id_type=MESH)
    for k in range(1, n_col):
        pl.semaphore_signal(barrier, inc=1, device_id={"col": lax.rem(c + k, n_col)}, device_id_type=MESH)

    sub8 = lax.broadcasted_iota(jnp.int32, (slots, LANES), 0)
    lane8 = lax.broadcasted_iota(jnp.int32, (slots, LANES), 1)
    old_tile = jnp.zeros((slots, LANES), jnp.int32)
    new_tile = jnp.full((slots, LANES), -1, jnp.int32)
    for s in range(slots):
        old_tile = jnp.where(sub8 == s, old_ref[0, s], old_tile)
        new_tile = jnp.where(lane8 == s, new_ref[0, s], new_tile)
    ids[0] = old_tile
    ids[1] = new_tile

    loads[2].wait()
    table = table_ref[...]
    high = table.astype(jnp.bfloat16)
    halves[:, :width] = high
    halves[:, width:] = (table - high.astype(jnp.float32)).astype(jnp.bfloat16)
    loads[0].wait()
    loads[1].wait()

    pl.semaphore_wait(barrier, n_row - 1 + n_col - 1)

    order = far_first(n_row)
    id_copies = {}
    for q in order:
        id_copies[q] = pltpu.make_async_remote_copy(
            src_ref=ids, dst_ref=ids_in.at[q], send_sem=ids_sem.at[q], recv_sem=ids_rsem.at[q],
            device_id={"row": row_peer(r, q, n_row, 1)}, device_id_type=MESH,
        )
        id_copies[q].start()

    marks = (
        lax.broadcasted_iota(jnp.int32, (slots * group // 16, 16, LANES), 0) * 16
        + lax.broadcasted_iota(jnp.int32, (slots * group // 16, 16, LANES), 1)
    ).astype(jnp.float32).astype(jnp.bfloat16)
    offs_marks = (
        lax.broadcasted_iota(jnp.int32, (blk // 16, 16, LANES), 0) * 16
        + lax.broadcasted_iota(jnp.int32, (blk // 16, 16, LANES), 1)
    ).astype(jnp.float32).astype(jnp.bfloat16)
    lane = lax.broadcasted_iota(jnp.int32, (8, LANES), 1)
    sub = lax.broadcasted_iota(jnp.int32, (8, LANES), 0)
    in_group = sub + (lane // bag) * 8
    in_bag = lax.broadcasted_iota(jnp.int32, (8, bag), 1)
    shift = blk.bit_length() - 1
    one = jnp.ones((), jnp.bfloat16)
    zero = jnp.zeros((), jnp.bfloat16)

    def spread(row, against):
        wide = jnp.broadcast_to(row, (16, LANES)).astype(jnp.bfloat16)
        hit = jnp.where(against == wide[None], one, zero)
        return hit.reshape(against.shape[0] * 16, LANES)

    def count_group(first, g):
        base = pl.multiple_of(first + g * group, group)
        picked = []
        for i in range(pack):
            rows = pl.ds(base + 8 * i, 8)
            picked.append(jnp.where(in_bag < len_ref[rows, :], idx_ref[rows, :], -1))
        wanted = jnp.concatenate(picked, axis=1)
        block = lax.shift_right_arithmetic(wanted, shift)
        off = (wanted & (blk - 1)).astype(jnp.float32)
        slot = jnp.full((8, LANES), -1, jnp.int32)
        for s in range(slots):
            slot = jnp.where(block == old_ref[0, s], s, slot)
        code = jnp.where(slot >= 0, slot * group + in_group, -1).astype(jnp.float32)
        a = jnp.concatenate([spread(code[j : j + 1], marks) for j in range(8)], axis=1)
        b = jnp.concatenate([spread(off[j : j + 1], offs_marks) for j in range(8)], axis=1)
        n = lax.dot_general(a, b, (((1,), (1,)), ((), ())), preferred_element_type=jnp.float32)
        n = n.astype(jnp.bfloat16)
        at = pl.ds(pl.multiple_of(g * group, group), group)
        for s in range(slots):
            counts[at, s * blk : (s + 1) * blk] = n[s * group : (s + 1) * group]

    def pool_chunk(q, dest):
        def pool_tile(t):
            first = dest * share + t * tile

            def body(g, carry):
                count_group(first, g)
                return carry

            lax.fori_loop(0, tile // group, body, 0)
            both = jnp.dot(counts[...], halves[...], preferred_element_type=jnp.float32)
            if isinstance(t, int):
                part[q, t * tile : (t + 1) * tile] = both[:, :width] + both[:, width:]
            else:
                part[q, pl.ds(pl.multiple_of(t * tile, tile), tile)] = both[:, :width] + both[:, width:]

        if share == tile:
            pool_tile(0)
        else:
            def step(t, carry):
                pool_tile(t)
                return carry

            lax.fori_loop(0, share // tile, step, 0)

    def send_part(q):
        copy = pltpu.make_async_remote_copy(
            src_ref=part.at[q], dst_ref=part_in.at[q], send_sem=part_sem.at[q], recv_sem=part_rsem.at[q],
            device_id={"row": row_peer(r, q, n_row, 1)}, device_id_type=MESH,
        )
        copy.start()
        return copy

    def send_blocks():
        copies = []
        for q in order:
            id_copies[q].wait()
        spots = {}
        for q in order + [0]:
            theirs = new_tile if q == 0 else ids_in[q, 1]
            codes = jnp.where(old_tile == theirs, lane8 * LANES + sub8, FAR)
            spots[q] = []
            for m in range(move):
                first = least(codes)
                spots[q].append(first & (LANES - 1))
                codes = jnp.where(codes > first, codes, FAR)
        for q in order + [0]:
            into = blocks_in if q == 0 else blocks_out
            for m in range(move):
                into[q, m] = choose(spots[q][m], [
                    functools.partial(lambda s: table_ref[s * blk : (s + 1) * blk, :], s)
                    for s in range(slots)
                ])
        for q in order:
            copy = pltpu.make_async_remote_copy(
                src_ref=blocks_out.at[q], dst_ref=blocks_in.at[q], send_sem=blk_sem.at[q], recv_sem=blk_rsem.at[q],
                device_id={"row": row_peer(r, q, n_row, 1)}, device_id_type=MESH,
            )
            copy.start()
            copies.append(copy)
        return copies

    copies = []
    for q in order:
        pool_chunk(q, row_peer(r, q, n_row, 1))
        copies.append(send_part(q))
    block_copies = send_blocks()
    pool_chunk(0, r)

    where_in = jnp.zeros((slots, LANES), jnp.int32)
    for q in range(n_row):
        theirs = old_tile if q == 0 else ids_in[q, 0]
        hit = theirs == new_tile
        codes = jnp.where(hit, lane8, FAR)
        rank = jnp.zeros((slots, LANES), jnp.int32)
        left = codes
        for m in range(move - 1):
            first = least(left)
            rank = rank + jnp.where(codes > first, 1, 0)
            left = jnp.where(left > first, left, FAR)
        where_in = where_in + jnp.where(hit, q * move + rank, 0)
    sources = [everywhere(jnp.sum, jnp.where(lane8 == p, where_in, 0)) for p in range(slots)]

    for copy in copies:
        copy.wait()
    acc = part[0]
    for q in range(1, n_row):
        acc = acc + part_in[q]
    total[...] = acc

    swaps = []
    for k in range(1, n_col):
        to = lax.rem(c + k, n_col)
        swap = pltpu.make_async_remote_copy(
            src_ref=total.at[pl.ds(pl.multiple_of(to * each, each), each)], dst_ref=swap_in.at[c],
            send_sem=swap_sem.at[k], recv_sem=swap_rsem.at[k],
            device_id={"col": to}, device_id_type=MESH,
        )
        swap.start()
        swaps.append(swap)
    mine = total[pl.ds(pl.multiple_of(c * each, each), each), :]

    for copy in block_copies:
        copy.wait()
    for p in range(slots):
        out_ref[p * blk : (p + 1) * blk, :] = choose(sources[p], [
            functools.partial(lambda q, m: blocks_in[q, m], q, m)
            for q in range(n_row) for m in range(move)
        ])
    for swap in swaps:
        swap.wait()
    pooled_ref[...] = swap_in[...]
    pooled_ref[c] = mine


def move_and_pool(n_row, n_col, old_blocks, new_blocks, table, wanted, lengths):
    rows, width = table.shape
    slots = old_blocks.shape[1]
    blk = rows // slots
    samples, bag = wanted.shape
    share = samples // n_row
    each = share // n_col
    move = slots // n_row
    hbm = pl.BlockSpec(memory_space=pl.ANY)
    smem = pl.BlockSpec(memory_space=pltpu.SMEM)
    vmem = pl.BlockSpec(memory_space=pltpu.VMEM)
    dma = pltpu.SemaphoreType.DMA
    return pl.pallas_call(
        functools.partial(kernel, n_row, n_col),
        out_shape=(
            jax.ShapeDtypeStruct((rows, width), jnp.float32),
            jax.ShapeDtypeStruct((n_col, each, width), jnp.float32),
        ),
        in_specs=[smem, smem, hbm, hbm, hbm],
        out_specs=(vmem, vmem),
        scratch_shapes=[
            pltpu.VMEM((rows, width), jnp.float32),
            pltpu.VMEM((samples, bag), jnp.int32),
            pltpu.VMEM((samples, 1), jnp.int32),
            pltpu.VMEM((2, slots, LANES), jnp.int32),
            pltpu.VMEM((n_row, 2, slots, LANES), jnp.int32),
            pltpu.VMEM((n_row, move, blk, width), jnp.float32),
            pltpu.VMEM((n_row, move, blk, width), jnp.float32),
            pltpu.VMEM((rows, 2 * width), jnp.bfloat16),
            pltpu.VMEM((min(share, 128), rows), jnp.bfloat16),
            pltpu.VMEM((n_row, share, width), jnp.float32),
            pltpu.VMEM((n_row, share, width), jnp.float32),
            pltpu.VMEM((share, width), jnp.float32),
            pltpu.VMEM((n_col, each, width), jnp.float32),
            dma((3,)),
            dma((n_row,)), dma((n_row,)),
            dma((n_row,)), dma((n_row,)),
            dma((n_row,)), dma((n_row,)),
            dma((n_col,)), dma((n_col,)),
        ],
        compiler_params=pltpu.CompilerParams(collective_id=0, has_side_effects=True),
    )(old_blocks, new_blocks, table, wanted, lengths)


def shards(
    old_table, old_blocks, new_blocks, bag_row_index, bag_length, dense, w_first, w_second, w_out
):
    width = old_table.shape[2]
    n_row, n_col = lax.axis_size("row"), lax.axis_size("col")
    new_table, pooled = move_and_pool(
        n_row, n_col, old_blocks, new_blocks, old_table[0], bag_row_index[:, 0, :], bag_length
    )
    dense_wide = dense.astype(jnp.float32)
    stacked = jnp.concatenate([dense_wide[None], pooled], axis=0)
    gram = jnp.einsum(
        "xcp,fcp->cxf", stacked, stacked, precision=lax.Precision.HIGHEST
    ) * width ** (-0.5)
    upper, lower = np.triu_indices(stacked.shape[0], 1)
    crossed = gram[:, upper, lower]
    joined = jnp.concatenate([dense_wide, crossed], axis=1).astype(jnp.bfloat16)
    hidden_one = jnp.maximum(
        jnp.dot(joined, w_first, preferred_element_type=jnp.float32), 0.0
    ).astype(jnp.bfloat16)
    hidden_two = jnp.maximum(
        jnp.dot(hidden_one, w_second, preferred_element_type=jnp.float32), 0.0
    ).astype(jnp.bfloat16)
    logits = jnp.dot(hidden_two, w_out, preferred_element_type=jnp.float32)
    return logits, new_table[None]


def solution(mesh):
    in_specs = (
        P("col", "row", None),
        P("col", "row"),
        P("col", "row"),
        P(None, "col", None),
        P(None, "col"),
        P(("row", "col"), None),
        P(),
        P(),
        P(),
    )
    out_specs = (P(("row", "col")), P("col", "row", None))
    return jax.shard_map(shards, mesh=mesh, in_specs=in_specs, out_specs=out_specs, check_vma=False)
```

```python
import functools

import jax
import jax.numpy as jnp
from jax import lax
from jax.experimental import pallas as pl
from jax.experimental.pallas import tpu as pltpu
from jax.sharding import PartitionSpec as P

MESH = pl.DeviceIdType.MESH
LANES = 128
FAR = 1 << 20
UNROLL = 1


def row_peer(r, q, n, sign):
    chips = n // 2
    return lax.rem(r // 2 + (sign * (q // 2)) % chips, chips) * 2 + lax.rem(r % 2 + q % 2, 2)


def far_first(n):
    return sorted(range(1, n), key=lambda q: -(q // 2))


def everywhere(reduce, x):
    return reduce(reduce(x, axis=1, keepdims=True), axis=0, keepdims=True)


def least(x):
    return everywhere(jnp.min, x)


def choose(which, reads):
    first = reads[0]()
    rows, width = first.shape
    wide = jnp.broadcast_to(which, (8, width))
    picked = first.reshape(rows // 8, 8, width)
    for at, read in enumerate(reads[1:], 1):
        picked = jnp.where((wide == at)[None], read().reshape(rows // 8, 8, width), picked)
    return picked.reshape(rows, width)


def kernel(
    n_row, n_col, scale,
    old_hbm, new_hbm, table_hbm, idx_hbm, len_hbm, dense_ref, first_hbm, second_hbm, last_ref,
    logits_ref, out_hbm,
    old_ref, new_ref, table_ref, idx_ref, len_ref, first_ref, second_ref, crossed_ref,
    ids, ids_in, blocks_out, blocks_in, arranged, halves, locs, counts,
    part, part_in, total, stack,
    load_sem, ids_sem, ids_rsem, blk_sem, blk_rsem, part_sem, part_rsem, swap_sem, swap_rsem, out_sem,
):
    r, c = lax.axis_index("row"), lax.axis_index("col")
    slots = old_ref.shape[1]
    blk = table_ref.shape[0] // slots
    width = table_ref.shape[1]
    move = slots // n_row
    bag, samples = idx_ref.shape
    share = samples // n_row
    each = share // n_col
    pack = LANES // bag
    group = 8 * pack
    tile = LANES
    half = tile // pack

    loads = [
        pltpu.make_async_copy(old_hbm, old_ref, load_sem.at[0]),
        pltpu.make_async_copy(new_hbm, new_ref, load_sem.at[1]),
        pltpu.make_async_copy(table_hbm, table_ref, load_sem.at[2]),
        pltpu.make_async_copy(idx_hbm, idx_ref, load_sem.at[3]),
        pltpu.make_async_copy(len_hbm, len_ref, load_sem.at[4]),
        pltpu.make_async_copy(first_hbm, first_ref, load_sem.at[5]),
        pltpu.make_async_copy(second_hbm, second_ref, load_sem.at[6]),
    ]
    for load in loads:
        load.start()

    barrier = pltpu.get_barrier_semaphore()
    for k in range(1, n_col):
        pl.semaphore_signal(barrier, inc=1, device_id={"col": lax.rem(c + k, n_col)}, device_id_type=MESH)
    for q in range(1, n_row):
        pl.semaphore_signal(barrier, inc=1, device_id={"row": row_peer(r, q, n_row, 1)}, device_id_type=MESH)

    loads[0].wait()
    loads[1].wait()
    sub8 = lax.broadcasted_iota(jnp.int32, (slots, LANES), 0)
    lane8 = lax.broadcasted_iota(jnp.int32, (slots, LANES), 1)
    old_tile = jnp.zeros((slots, LANES), jnp.int32)
    new_tile = jnp.full((slots, LANES), -1, jnp.int32)
    for s in range(slots):
        old_tile = jnp.where(sub8 == s, old_ref[0, s], old_tile)
        new_tile = jnp.where(lane8 == s, new_ref[0, s], new_tile)
    ids[0] = old_tile
    ids[1] = new_tile

    loads[2].wait()
    table = table_ref[...]
    high = table.astype(jnp.bfloat16)
    halves[:, :width] = high
    halves[:, width:] = (table - high.astype(jnp.float32)).astype(jnp.bfloat16)
    loads[3].wait()
    loads[4].wait()

    marks = (
        lax.broadcasted_iota(jnp.int32, (slots * group // 16, 16, LANES), 0) * 16
        + lax.broadcasted_iota(jnp.int32, (slots * group // 16, 16, LANES), 1)
    ).astype(jnp.float32).astype(jnp.bfloat16)
    offs_marks = (
        lax.broadcasted_iota(jnp.int32, (blk // 16, 16, LANES), 0) * 16
        + lax.broadcasted_iota(jnp.int32, (blk // 16, 16, LANES), 1)
    ).astype(jnp.float32).astype(jnp.bfloat16)
    lane = lax.broadcasted_iota(jnp.int32, (8, LANES), 1)
    sub = lax.broadcasted_iota(jnp.int32, (8, LANES), 0)
    in_group = sub + (lane // bag) * 8
    in_bag = lax.broadcasted_iota(jnp.int32, (bag, tile), 0)
    shift = blk.bit_length() - 1
    one = jnp.ones((), jnp.bfloat16)
    zero = jnp.zeros((), jnp.bfloat16)

    def spread(row, against):
        wide = jnp.broadcast_to(row, (16, LANES)).astype(jnp.bfloat16)
        hit = jnp.where(against == wide[None], one, zero)
        return hit.reshape(against.shape[0] * 16, LANES)

    def locate(first):
        bags = pl.ds(pl.multiple_of(first, tile), tile)
        wanted = jnp.where(in_bag < len_ref[:, bags], idx_ref[:, bags], -1)
        block = lax.shift_right_arithmetic(wanted, shift)
        off = wanted & (blk - 1)
        loc = jnp.full((bag, tile), -1, jnp.int32)
        for s in range(slots):
            loc = jnp.where(block == old_ref[0, s], off + s * blk, loc)
        turned = loc.astype(jnp.float32).T
        locs[...] = jnp.concatenate(
            [turned[i * half : (i + 1) * half] for i in range(pack)], axis=1
        ).astype(jnp.int32)

    def count_group(g):
        loc = locs[pl.ds(pl.multiple_of(g * 8, 8), 8), :]
        off = (loc & (blk - 1)).astype(jnp.float32)
        code = jnp.where(
            loc >= 0, lax.shift_right_arithmetic(loc, shift) * group + in_group, -1
        ).astype(jnp.float32)
        a = jnp.concatenate([spread(code[j : j + 1], marks) for j in range(8)], axis=1)
        b = jnp.concatenate([spread(off[j : j + 1], offs_marks) for j in range(8)], axis=1)
        n = lax.dot_general(a, b, (((1,), (1,)), ((), ())), preferred_element_type=jnp.float32)
        n = n.astype(jnp.bfloat16)
        at = pl.ds(pl.multiple_of(g * group, group), group)
        for s in range(slots):
            counts[at, s * blk : (s + 1) * blk] = n[s * group : (s + 1) * group]

    def pool_chunk(q, dest):
        def pool_tile(t):
            locate(dest * share + t * tile)

            def body(g, carry):
                count_group(g)
                return carry

            lax.fori_loop(0, tile // group, body, 0, unroll=UNROLL)
            both = jnp.dot(counts[...], halves[...], preferred_element_type=jnp.float32)
            both = both[:, :width] + both[:, width:]
            for i in range(tile // 8):
                g, j = i // pack, i % pack
                at = pl.multiple_of(t * tile + j * half + g * 8, 8)
                part[q, pl.ds(at, 8)] = both[i * 8 : (i + 1) * 8]

        if share == tile:
            pool_tile(0)
        else:
            def step(t, carry):
                pool_tile(t)
                return carry

            lax.fori_loop(0, share // tile, step, 0)

    order = far_first(n_row)
    far = [q for q in order if q // 2]
    near = [q for q in order if not q // 2]

    def to_row(q, src, dst, sems, rsems):
        copy = pltpu.make_async_remote_copy(
            src_ref=src, dst_ref=dst, send_sem=sems.at[q], recv_sem=rsems.at[q],
            device_id={"row": row_peer(r, q, n_row, 1)}, device_id_type=MESH,
        )
        copy.start()
        return copy

    def pick_blocks(q):
        theirs = new_tile if q == 0 else ids_in[q, 1]
        into = blocks_in if q == 0 else blocks_out
        codes = jnp.where(old_tile == theirs, lane8 * LANES + sub8, FAR)
        for m in range(move):
            first = least(codes)
            codes = jnp.where(codes > first, codes, FAR)
            into[q, m] = choose(first & (LANES - 1), [
                functools.partial(lambda s: table_ref[s * blk : (s + 1) * blk, :], s)
                for s in range(slots)
            ])

    part_copies, id_copies, block_copies = [], {}, []
    pool_chunk(order[0], row_peer(r, order[0], n_row, 1))
    pl.semaphore_wait(barrier, n_row - 1 + n_col - 1)
    for q in order:
        id_copies[q] = to_row(q, ids, ids_in.at[q], ids_sem, ids_rsem)
    part_copies.append(to_row(order[0], part.at[order[0]], part_in.at[order[0]], part_sem, part_rsem))
    for q in far[1:]:
        pool_chunk(q, row_peer(r, q, n_row, 1))
        part_copies.append(to_row(q, part.at[q], part_in.at[q], part_sem, part_rsem))
    for q in order:
        id_copies[q].wait()
    for q in far:
        pick_blocks(q)
        block_copies.append(to_row(q, blocks_out.at[q], blocks_in.at[q], blk_sem, blk_rsem))
    for q in near:
        pool_chunk(q, row_peer(r, q, n_row, 1))
        part_copies.append(to_row(q, part.at[q], part_in.at[q], part_sem, part_rsem))
        pick_blocks(q)
        block_copies.append(to_row(q, blocks_out.at[q], blocks_in.at[q], blk_sem, blk_rsem))
    pool_chunk(0, r)
    pick_blocks(0)

    where_in = jnp.zeros((slots, LANES), jnp.int32)
    for q in range(n_row):
        theirs = old_tile if q == 0 else ids_in[q, 0]
        hit = theirs == new_tile
        codes = jnp.where(hit, lane8, FAR)
        rank = jnp.zeros((slots, LANES), jnp.int32)
        left = codes
        for m in range(move - 1):
            first = least(left)
            rank = rank + jnp.where(codes > first, 1, 0)
            left = jnp.where(left > first, left, FAR)
        where_in = where_in + jnp.where(hit, q * move + rank, 0)
    sources = [everywhere(jnp.sum, jnp.where(lane8 == p, where_in, 0)) for p in range(slots)]

    for copy in part_copies:
        copy.wait()
    acc = part[0]
    for q in range(1, n_row):
        acc = acc + part_in[q]
    total[...] = acc

    swaps = []
    for k in range(1, n_col):
        to = lax.rem(c + k, n_col)
        swap = pltpu.make_async_remote_copy(
            src_ref=total.at[pl.ds(pl.multiple_of(to * each, each), each)], dst_ref=stack.at[c + 1],
            send_sem=swap_sem.at[k], recv_sem=swap_rsem.at[k],
            device_id={"col": to}, device_id_type=MESH,
        )
        swap.start()
        swaps.append(swap)
    stack[0] = dense_ref[...].astype(jnp.float32)
    stack[c + 1] = total[pl.ds(pl.multiple_of(c * each, each), each), :]
    crossed_ref[...] = jnp.zeros_like(crossed_ref)
    lanes = lax.broadcasted_iota(jnp.int32, (each, LANES), 1)
    loads[5].wait()
    loads[6].wait()
    for swap in swaps:
        swap.wait()

    count = n_col + 1
    pairs = count * (count - 1) // 2
    if pairs <= LANES:
        crossed = jnp.zeros((each, LANES), jnp.float32)
        k = 0
        for i in range(count):
            for j in range(i + 1, count):
                dot = jnp.sum(stack[i] * stack[j], axis=1, keepdims=True) * scale
                crossed = jnp.where(lanes == k, dot, crossed)
                k += 1
        crossed_ref[...] = crossed
    else:
        def rows(i, k):
            def cols(j, k):
                dot = jnp.sum(stack[i] * stack[j], axis=1, keepdims=True) * scale
                at = pl.ds(pl.multiple_of(k // LANES * LANES, LANES), LANES)
                crossed_ref[:, at] = jnp.where(lanes == k % LANES, dot, crossed_ref[:, at])
                return k + 1

            return lax.fori_loop(i + 1, count, cols, k)

        lax.fori_loop(0, count, rows, 0)
    crossed = crossed_ref[...].astype(jnp.bfloat16)[:, :pairs]
    hidden = jnp.dot(dense_ref[...], first_ref[:width, :], preferred_element_type=jnp.float32)
    hidden = hidden + jnp.dot(crossed, first_ref[width:, :], preferred_element_type=jnp.float32)
    hidden = jnp.maximum(hidden, 0.0).astype(jnp.bfloat16)
    hidden = jnp.dot(hidden, second_ref[...], preferred_element_type=jnp.float32)
    hidden = jnp.maximum(hidden, 0.0).astype(jnp.bfloat16).astype(jnp.float32)
    last = last_ref[...].astype(jnp.float32)
    acc = jnp.zeros((each, LANES), jnp.float32)
    for j in range(last.shape[0]):
        acc = acc + hidden[:, j * LANES : (j + 1) * LANES] * last[j : j + 1, :]
    logit = jnp.sum(acc, axis=1, keepdims=True)
    subs = lax.broadcasted_iota(jnp.int32, (each, LANES), 0)
    logits_ref[...] = jnp.sum(jnp.where(subs == lanes, logit, 0.0), axis=0, keepdims=True)[:, :each]

    for copy in block_copies:
        copy.wait()
    outs = []
    for p in range(slots):
        arranged[p] = choose(sources[p], [
            functools.partial(lambda q, m: blocks_in[q, m], q, m)
            for q in range(n_row) for m in range(move)
        ])
        out = pltpu.make_async_copy(arranged.at[p], out_hbm.at[pl.ds(p * blk, blk)], out_sem.at[p])
        out.start()
        outs.append(out)
    for out in outs:
        out.wait()


def step(n_row, n_col, old_blocks, new_blocks, table, wanted, lengths, dense, w_first, w_second, w_out):
    rows, width = table.shape
    slots = old_blocks.shape[1]
    blk = rows // slots
    bag, samples = wanted.shape
    share = samples // n_row
    each = share // n_col
    move = slots // n_row
    hbm = pl.BlockSpec(memory_space=pl.ANY)
    vmem = pl.BlockSpec(memory_space=pltpu.VMEM)
    dma = pltpu.SemaphoreType.DMA
    pairs = n_col * (n_col + 1) // 2
    return pl.pallas_call(
        functools.partial(kernel, n_row, n_col, width ** (-0.5)),
        out_shape=(
            jax.ShapeDtypeStruct((1, each), jnp.float32),
            jax.ShapeDtypeStruct((rows, width), jnp.float32),
        ),
        in_specs=[hbm, hbm, hbm, hbm, hbm, vmem, hbm, hbm, vmem],
        out_specs=(vmem, hbm),
        scratch_shapes=[
            pltpu.SMEM(old_blocks.shape, jnp.int32),
            pltpu.SMEM(new_blocks.shape, jnp.int32),
            pltpu.VMEM((rows, width), jnp.float32),
            pltpu.VMEM(wanted.shape, jnp.int32),
            pltpu.VMEM(lengths.shape, jnp.int32),
            pltpu.VMEM(w_first.shape, jnp.bfloat16),
            pltpu.VMEM(w_second.shape, jnp.bfloat16),
            pltpu.VMEM((each, -(-pairs // LANES) * LANES), jnp.float32),
            pltpu.VMEM((2, slots, LANES), jnp.int32),
            pltpu.VMEM((n_row, 2, slots, LANES), jnp.int32),
            pltpu.VMEM((n_row, move, blk, width), jnp.float32),
            pltpu.VMEM((n_row, move, blk, width), jnp.float32),
            pltpu.VMEM((slots, blk, width), jnp.float32),
            pltpu.VMEM((rows, 2 * width), jnp.bfloat16),
            pltpu.VMEM((bag, LANES), jnp.int32),
            pltpu.VMEM((LANES, rows), jnp.bfloat16),
            pltpu.VMEM((n_row, share, width), jnp.float32),
            pltpu.VMEM((n_row, share, width), jnp.float32),
            pltpu.VMEM((share, width), jnp.float32),
            pltpu.VMEM((n_col + 1, each, width), jnp.float32),
            dma((7,)),
            dma((n_row,)), dma((n_row,)),
            dma((n_row,)), dma((n_row,)),
            dma((n_row,)), dma((n_row,)),
            dma((n_col,)), dma((n_col,)),
            dma((slots,)),
        ],
        compiler_params=pltpu.CompilerParams(collective_id=0, has_side_effects=True),
    )(old_blocks, new_blocks, table, wanted, lengths, dense, w_first, w_second, w_out)


def shards(
    old_table, old_blocks, new_blocks, bag_row_index, bag_length, dense, w_first, w_second, w_out
):
    n_row, n_col = lax.axis_size("row"), lax.axis_size("col")
    logits, new_table = step(
        n_row, n_col, old_blocks, new_blocks, old_table[0], bag_row_index[:, 0, :].T, bag_length.T,
        dense, w_first, w_second, w_out.reshape(-1, LANES),
    )
    return logits.reshape(-1), new_table[None]


def solution(mesh):
    in_specs = (
        P("col", "row", None),
        P("col", "row"),
        P("col", "row"),
        P(None, "col", None),
        P(None, "col"),
        P(("row", "col"), None),
        P(),
        P(),
        P(),
    )
    out_specs = (P(("row", "col")), P("col", "row", None))
    return jax.shard_map(shards, mesh=mesh, in_specs=in_specs, out_specs=out_specs, check_vma=False)
```

```python
import functools

import jax
import jax.numpy as jnp
from jax import lax
from jax.experimental import pallas as pl
from jax.experimental.pallas import tpu as pltpu
from jax.sharding import PartitionSpec as P

MESH = pl.DeviceIdType.MESH
LANES = 128
FAR = 1 << 20
UNROLL = 4


def row_peer(r, q, n, sign):
    chips = n // 2
    return lax.rem(r // 2 + (sign * (q // 2)) % chips, chips) * 2 + lax.rem(r % 2 + q % 2, 2)


def far_first(n):
    return sorted(range(1, n), key=lambda q: -(q // 2))


def everywhere(reduce, x):
    return reduce(reduce(x, axis=1, keepdims=True), axis=0, keepdims=True)


def least(x):
    return everywhere(jnp.min, x)


def choose(which, reads):
    first = reads[0]()
    rows, width = first.shape
    wide = jnp.broadcast_to(which, (8, width))
    picked = first.reshape(rows // 8, 8, width)
    for at, read in enumerate(reads[1:], 1):
        picked = jnp.where((wide == at)[None], read().reshape(rows // 8, 8, width), picked)
    return picked.reshape(rows, width)


def kernel(
    n_row, n_col, scale,
    old_hbm, new_hbm, table_hbm, idx_hbm, len_hbm, dense_ref, first_hbm, second_hbm, last_ref,
    logits_ref, spots_ref, blocks_in,
    old_ref, new_ref, table_ref, idx_ref, len_ref, first_ref, second_ref, crossed_ref,
    ids, ids_in, blocks_out, halves, locs, counts,
    part, part_in, total, stack,
    load_sem, ids_sem, ids_rsem, blk_sem, blk_rsem, part_sem, part_rsem, swap_sem, swap_rsem,
):
    r, c = lax.axis_index("row"), lax.axis_index("col")
    slots = old_ref.shape[1]
    blk = table_ref.shape[0] // slots
    width = table_ref.shape[1]
    move = slots // n_row
    bag, samples = idx_ref.shape
    share = samples // n_row
    each = share // n_col
    pack = LANES // bag
    group = 8 * pack
    tile = LANES
    half = tile // pack

    loads = [
        pltpu.make_async_copy(old_hbm, old_ref, load_sem.at[0]),
        pltpu.make_async_copy(new_hbm, new_ref, load_sem.at[1]),
        pltpu.make_async_copy(table_hbm, table_ref, load_sem.at[2]),
        pltpu.make_async_copy(idx_hbm, idx_ref, load_sem.at[3]),
        pltpu.make_async_copy(len_hbm, len_ref, load_sem.at[4]),
        pltpu.make_async_copy(first_hbm, first_ref, load_sem.at[5]),
        pltpu.make_async_copy(second_hbm, second_ref, load_sem.at[6]),
    ]
    for load in loads:
        load.start()

    barrier = pltpu.get_barrier_semaphore()
    for k in range(1, n_col):
        pl.semaphore_signal(barrier, inc=1, device_id={"col": lax.rem(c + k, n_col)}, device_id_type=MESH)
    for q in range(1, n_row):
        pl.semaphore_signal(barrier, inc=1, device_id={"row": row_peer(r, q, n_row, 1)}, device_id_type=MESH)

    loads[0].wait()
    loads[1].wait()
    sub8 = lax.broadcasted_iota(jnp.int32, (slots, LANES), 0)
    lane8 = lax.broadcasted_iota(jnp.int32, (slots, LANES), 1)
    old_tile = jnp.zeros((slots, LANES), jnp.int32)
    new_tile = jnp.full((slots, LANES), -1, jnp.int32)
    for s in range(slots):
        old_tile = jnp.where(sub8 == s, old_ref[0, s], old_tile)
        new_tile = jnp.where(lane8 == s, new_ref[0, s], new_tile)
    ids[0] = old_tile
    ids[1] = new_tile

    loads[2].wait()
    table = table_ref[...]
    high = table.astype(jnp.bfloat16)
    halves[:, :width] = high
    halves[:, width:] = (table - high.astype(jnp.float32)).astype(jnp.bfloat16)
    loads[3].wait()
    loads[4].wait()

    marks = (
        lax.broadcasted_iota(jnp.int32, (slots * group // 16, 16, LANES), 0) * 16
        + lax.broadcasted_iota(jnp.int32, (slots * group // 16, 16, LANES), 1)
    ).astype(jnp.float32).astype(jnp.bfloat16)
    offs_marks = (
        lax.broadcasted_iota(jnp.int32, (blk // 16, 16, LANES), 0) * 16
        + lax.broadcasted_iota(jnp.int32, (blk // 16, 16, LANES), 1)
    ).astype(jnp.float32).astype(jnp.bfloat16)
    lane = lax.broadcasted_iota(jnp.int32, (8, LANES), 1)
    sub = lax.broadcasted_iota(jnp.int32, (8, LANES), 0)
    in_group = sub + (lane // bag) * 8
    in_bag = lax.broadcasted_iota(jnp.int32, (bag, tile), 0)
    shift = blk.bit_length() - 1
    one = jnp.ones((), jnp.bfloat16)
    zero = jnp.zeros((), jnp.bfloat16)

    def spread(row, against):
        wide = jnp.broadcast_to(row, (16, LANES)).astype(jnp.bfloat16)
        hit = jnp.where(against == wide[None], one, zero)
        return hit.reshape(against.shape[0] * 16, LANES)

    def locate(first):
        bags = pl.ds(pl.multiple_of(first, tile), tile)
        wanted = jnp.where(in_bag < len_ref[:, bags], idx_ref[:, bags], -1)
        block = lax.shift_right_arithmetic(wanted, shift)
        off = wanted & (blk - 1)
        loc = jnp.full((bag, tile), -1, jnp.int32)
        for s in range(slots):
            loc = jnp.where(block == old_ref[0, s], off + s * blk, loc)
        turned = loc.astype(jnp.float32).T
        locs[...] = jnp.concatenate(
            [turned[i * half : (i + 1) * half] for i in range(pack)], axis=1
        ).astype(jnp.int32)

    def count_group(g):
        loc = locs[pl.ds(pl.multiple_of(g * 8, 8), 8), :]
        off = (loc & (blk - 1)).astype(jnp.float32)
        code = jnp.where(
            loc >= 0, lax.shift_right_arithmetic(loc, shift) * group + in_group, -1
        ).astype(jnp.float32)
        a = jnp.concatenate([spread(code[j : j + 1], marks) for j in range(8)], axis=1)
        b = jnp.concatenate([spread(off[j : j + 1], offs_marks) for j in range(8)], axis=1)
        n = lax.dot_general(a, b, (((1,), (1,)), ((), ())), preferred_element_type=jnp.float32)
        n = n.astype(jnp.bfloat16)
        at = pl.ds(pl.multiple_of(g * group, group), group)
        for s in range(slots):
            counts[at, s * blk : (s + 1) * blk] = n[s * group : (s + 1) * group]

    def pool_chunk(q, dest):
        def pool_tile(t):
            locate(dest * share + t * tile)

            def body(g, carry):
                count_group(g)
                return carry

            lax.fori_loop(0, tile // group, body, 0, unroll=UNROLL)
            both = jnp.dot(counts[...], halves[...], preferred_element_type=jnp.float32)
            both = both[:, :width] + both[:, width:]
            for i in range(tile // 8):
                g, j = i // pack, i % pack
                at = pl.multiple_of(t * tile + j * half + g * 8, 8)
                part[q, pl.ds(at, 8)] = both[i * 8 : (i + 1) * 8]

        if share == tile:
            pool_tile(0)
        else:
            def step(t, carry):
                pool_tile(t)
                return carry

            lax.fori_loop(0, share // tile, step, 0)

    order = far_first(n_row)
    far = [q for q in order if q // 2]
    near = [q for q in order if not q // 2]

    def to_row(q, src, dst, sems, rsems):
        copy = pltpu.make_async_remote_copy(
            src_ref=src, dst_ref=dst, send_sem=sems.at[q], recv_sem=rsems.at[q],
            device_id={"row": row_peer(r, q, n_row, 1)}, device_id_type=MESH,
        )
        copy.start()
        return copy

    def pick_blocks(q):
        theirs = new_tile if q == 0 else ids_in[q, 1]
        into = blocks_in if q == 0 else blocks_out
        codes = jnp.where(old_tile == theirs, lane8 * LANES + sub8, FAR)
        for m in range(move):
            first = least(codes)
            codes = jnp.where(codes > first, codes, FAR)
            into[q * move + m] = choose(first & (LANES - 1), [
                functools.partial(lambda s: table_ref[s * blk : (s + 1) * blk, :], s)
                for s in range(slots)
            ])

    part_copies, id_copies, block_copies = [], {}, []
    pool_chunk(order[0], row_peer(r, order[0], n_row, 1))
    pl.semaphore_wait(barrier, n_row - 1 + n_col - 1)
    for q in order:
        id_copies[q] = to_row(q, ids, ids_in.at[q], ids_sem, ids_rsem)
    part_copies.append(to_row(order[0], part.at[order[0]], part_in.at[order[0]], part_sem, part_rsem))
    for q in far[1:]:
        pool_chunk(q, row_peer(r, q, n_row, 1))
        part_copies.append(to_row(q, part.at[q], part_in.at[q], part_sem, part_rsem))
    for q in order:
        id_copies[q].wait()
    for q in far:
        pick_blocks(q)
        block_copies.append(to_row(q, blocks_out.at[pl.ds(q * move, move)], blocks_in.at[pl.ds(q * move, move)], blk_sem, blk_rsem))
    for q in near:
        pool_chunk(q, row_peer(r, q, n_row, 1))
        part_copies.append(to_row(q, part.at[q], part_in.at[q], part_sem, part_rsem))
        pick_blocks(q)
        block_copies.append(to_row(q, blocks_out.at[pl.ds(q * move, move)], blocks_in.at[pl.ds(q * move, move)], blk_sem, blk_rsem))
    pool_chunk(0, r)
    pick_blocks(0)

    where_in = jnp.zeros((slots, LANES), jnp.int32)
    for q in range(n_row):
        theirs = old_tile if q == 0 else ids_in[q, 0]
        hit = theirs == new_tile
        codes = jnp.where(hit, lane8, FAR)
        rank = jnp.zeros((slots, LANES), jnp.int32)
        left = codes
        for m in range(move - 1):
            first = least(left)
            rank = rank + jnp.where(codes > first, 1, 0)
            left = jnp.where(left > first, left, FAR)
        where_in = where_in + jnp.where(hit, q * move + rank, 0)
    spots_ref[...] = jnp.sum(where_in, axis=0, keepdims=True)

    for copy in part_copies:
        copy.wait()
    acc = part[0]
    for q in range(1, n_row):
        acc = acc + part_in[q]
    total[...] = acc

    swaps = []
    for k in range(1, n_col):
        to = lax.rem(c + k, n_col)
        swap = pltpu.make_async_remote_copy(
            src_ref=total.at[pl.ds(pl.multiple_of(to * each, each), each)], dst_ref=stack.at[c + 1],
            send_sem=swap_sem.at[k], recv_sem=swap_rsem.at[k],
            device_id={"col": to}, device_id_type=MESH,
        )
        swap.start()
        swaps.append(swap)
    stack[0] = dense_ref[...].astype(jnp.float32)
    stack[c + 1] = total[pl.ds(pl.multiple_of(c * each, each), each), :]
    crossed_ref[...] = jnp.zeros_like(crossed_ref)
    lanes = lax.broadcasted_iota(jnp.int32, (each, LANES), 1)
    loads[5].wait()
    loads[6].wait()
    for swap in swaps:
        swap.wait()

    count = n_col + 1
    pairs = count * (count - 1) // 2
    if pairs <= LANES:
        crossed = jnp.zeros((each, LANES), jnp.float32)
        k = 0
        for i in range(count):
            for j in range(i + 1, count):
                dot = jnp.sum(stack[i] * stack[j], axis=1, keepdims=True) * scale
                crossed = jnp.where(lanes == k, dot, crossed)
                k += 1
        crossed_ref[...] = crossed
    else:
        def rows(i, k):
            def cols(j, k):
                dot = jnp.sum(stack[i] * stack[j], axis=1, keepdims=True) * scale
                at = pl.ds(pl.multiple_of(k // LANES * LANES, LANES), LANES)
                crossed_ref[:, at] = jnp.where(lanes == k % LANES, dot, crossed_ref[:, at])
                return k + 1

            return lax.fori_loop(i + 1, count, cols, k)

        lax.fori_loop(0, count, rows, 0)
    crossed = crossed_ref[...].astype(jnp.bfloat16)[:, :pairs]
    hidden = jnp.dot(dense_ref[...], first_ref[:width, :], preferred_element_type=jnp.float32)
    hidden = hidden + jnp.dot(crossed, first_ref[width:, :], preferred_element_type=jnp.float32)
    hidden = jnp.maximum(hidden, 0.0).astype(jnp.bfloat16)
    hidden = jnp.dot(hidden, second_ref[...], preferred_element_type=jnp.float32)
    hidden = jnp.maximum(hidden, 0.0).astype(jnp.bfloat16).astype(jnp.float32)
    last = last_ref[...].astype(jnp.float32)
    acc = jnp.zeros((each, LANES), jnp.float32)
    for j in range(last.shape[0]):
        acc = acc + hidden[:, j * LANES : (j + 1) * LANES] * last[j : j + 1, :]
    logit = jnp.sum(acc, axis=1, keepdims=True)
    subs = lax.broadcasted_iota(jnp.int32, (each, LANES), 0)
    logits_ref[...] = jnp.sum(jnp.where(subs == lanes, logit, 0.0), axis=0, keepdims=True)[:, :each]

    for copy in block_copies:
        copy.wait()


def arrange(spots, logits_in, blocks, logits_ref, out_hbm, sems):
    count, blk = blocks.shape[:2]
    copies = [
        pltpu.make_async_copy(blocks.at[spots[0, p]], out_hbm.at[pl.ds(p * blk, blk)], sems.at[p])
        for p in range(count)
    ]
    for copy in copies:
        copy.start()
    logits_ref[...] = logits_in[...]
    for copy in copies:
        copy.wait()


def step(n_row, n_col, old_blocks, new_blocks, table, wanted, lengths, dense, w_first, w_second, w_out):
    rows, width = table.shape
    slots = old_blocks.shape[1]
    blk = rows // slots
    bag, samples = wanted.shape
    share = samples // n_row
    each = share // n_col
    move = slots // n_row
    hbm = pl.BlockSpec(memory_space=pl.ANY)
    vmem = pl.BlockSpec(memory_space=pltpu.VMEM)
    dma = pltpu.SemaphoreType.DMA
    pairs = n_col * (n_col + 1) // 2
    logits, spots, blocks = pl.pallas_call(
        functools.partial(kernel, n_row, n_col, width ** (-0.5)),
        out_shape=(
            jax.ShapeDtypeStruct((1, each), jnp.float32),
            jax.ShapeDtypeStruct((1, LANES), jnp.int32),
            pltpu.VMEM((slots, blk, width), jnp.float32),
        ),
        in_specs=[hbm, hbm, hbm, hbm, hbm, vmem, hbm, hbm, vmem],
        out_specs=(vmem, vmem, vmem),
        scratch_shapes=[
            pltpu.SMEM(old_blocks.shape, jnp.int32),
            pltpu.SMEM(new_blocks.shape, jnp.int32),
            pltpu.VMEM((rows, width), jnp.float32),
            pltpu.VMEM(wanted.shape, jnp.int32),
            pltpu.VMEM(lengths.shape, jnp.int32),
            pltpu.VMEM(w_first.shape, jnp.bfloat16),
            pltpu.VMEM(w_second.shape, jnp.bfloat16),
            pltpu.VMEM((each, -(-pairs // LANES) * LANES), jnp.float32),
            pltpu.VMEM((2, slots, LANES), jnp.int32),
            pltpu.VMEM((n_row, 2, slots, LANES), jnp.int32),
            pltpu.VMEM((slots, blk, width), jnp.float32),
            pltpu.VMEM((rows, 2 * width), jnp.bfloat16),
            pltpu.VMEM((bag, LANES), jnp.int32),
            pltpu.VMEM((LANES, rows), jnp.bfloat16),
            pltpu.VMEM((n_row, share, width), jnp.float32),
            pltpu.VMEM((n_row, share, width), jnp.float32),
            pltpu.VMEM((share, width), jnp.float32),
            pltpu.VMEM((n_col + 1, each, width), jnp.float32),
            dma((7,)),
            dma((n_row,)), dma((n_row,)),
            dma((n_row,)), dma((n_row,)),
            dma((n_row,)), dma((n_row,)),
            dma((n_col,)), dma((n_col,)),
        ],
        compiler_params=pltpu.CompilerParams(collective_id=0, has_side_effects=True),
    )(old_blocks, new_blocks, table, wanted, lengths, dense, w_first, w_second, w_out)
    return pl.pallas_call(
        arrange,
        out_shape=(
            jax.ShapeDtypeStruct((1, each), jnp.float32),
            jax.ShapeDtypeStruct((rows, width), jnp.float32),
        ),
        in_specs=[pl.BlockSpec(memory_space=pltpu.SMEM), vmem, hbm],
        out_specs=(vmem, hbm),
        scratch_shapes=[dma((slots,))],
    )(spots, logits, pltpu.with_memory_space_constraint(blocks, pltpu.VMEM))


def shards(
    old_table, old_blocks, new_blocks, bag_row_index, bag_length, dense, w_first, w_second, w_out
):
    n_row, n_col = lax.axis_size("row"), lax.axis_size("col")
    logits, new_table = step(
        n_row, n_col, old_blocks, new_blocks, old_table[0], bag_row_index[:, 0, :].T, bag_length.T,
        dense, w_first, w_second, w_out.reshape(-1, LANES),
    )
    return logits.reshape(-1), new_table[None]


def solution(mesh):
    in_specs = (
        P("col", "row", None),
        P("col", "row"),
        P("col", "row"),
        P(None, "col", None),
        P(None, "col"),
        P(("row", "col"), None),
        P(),
        P(),
        P(),
    )
    out_specs = (P(("row", "col")), P("col", "row", None))
    return jax.shard_map(shards, mesh=mesh, in_specs=in_specs, out_specs=out_specs, check_vma=False)
```

```python
import functools

import jax
import jax.numpy as jnp
from jax import lax
from jax.experimental import pallas as pl
from jax.experimental.pallas import tpu as pltpu
from jax.sharding import PartitionSpec as P

MESH = pl.DeviceIdType.MESH
LANES = 128
FAR = 1 << 20
UNROLL = 4


def row_peer(r, q, n, sign):
    chips = n // 2
    return lax.rem(r // 2 + (sign * (q // 2)) % chips, chips) * 2 + lax.rem(r % 2 + q % 2, 2)


def far_first(n):
    return sorted(range(1, n), key=lambda q: -(q // 2))


def everywhere(reduce, x):
    return reduce(reduce(x, axis=1, keepdims=True), axis=0, keepdims=True)


def least(x):
    return everywhere(jnp.min, x)


def choose(which, reads):
    first = reads[0]()
    rows, width = first.shape
    wide = jnp.broadcast_to(which, (8, width))
    picked = first.reshape(rows // 8, 8, width)
    for at, read in enumerate(reads[1:], 1):
        picked = jnp.where((wide == at)[None], read().reshape(rows // 8, 8, width), picked)
    return picked.reshape(rows, width)


def kernel(
    n_row, n_col, scale,
    old_hbm, new_hbm, table_hbm, idx_hbm, len_hbm, dense_ref, first_hbm, second_hbm, last_ref,
    logits_ref, arranged,
    old_ref, new_ref, table_ref, idx_ref, len_ref, first_ref, second_ref, crossed_ref,
    ids, ids_in, blocks_out, blocks_in, halves, locs, counts,
    part, part_in, total, stack,
    load_sem, ids_sem, ids_rsem, blk_sem, blk_rsem, part_sem, part_rsem, swap_sem, swap_rsem,
):
    r, c = lax.axis_index("row"), lax.axis_index("col")
    slots = old_ref.shape[1]
    blk = table_ref.shape[0] // slots
    width = table_ref.shape[1]
    move = slots // n_row
    bag, samples = idx_ref.shape
    share = samples // n_row
    each = share // n_col
    pack = LANES // bag
    group = 8 * pack
    tile = LANES
    half = tile // pack

    loads = [
        pltpu.make_async_copy(old_hbm, old_ref, load_sem.at[0]),
        pltpu.make_async_copy(new_hbm, new_ref, load_sem.at[1]),
        pltpu.make_async_copy(table_hbm, table_ref, load_sem.at[2]),
        pltpu.make_async_copy(idx_hbm, idx_ref, load_sem.at[3]),
        pltpu.make_async_copy(len_hbm, len_ref, load_sem.at[4]),
        pltpu.make_async_copy(first_hbm, first_ref, load_sem.at[5]),
        pltpu.make_async_copy(second_hbm, second_ref, load_sem.at[6]),
    ]
    for load in [loads[3], loads[4], loads[0], loads[1], loads[2]]:
        load.start()

    barrier = pltpu.get_barrier_semaphore()
    for k in range(1, n_col):
        pl.semaphore_signal(barrier, inc=1, device_id={"col": lax.rem(c + k, n_col)}, device_id_type=MESH)
    for q in range(1, n_row):
        pl.semaphore_signal(barrier, inc=1, device_id={"row": row_peer(r, q, n_row, 1)}, device_id_type=MESH)

    loads[0].wait()
    loads[1].wait()
    sub8 = lax.broadcasted_iota(jnp.int32, (slots, LANES), 0)
    lane8 = lax.broadcasted_iota(jnp.int32, (slots, LANES), 1)
    old_tile = jnp.zeros((slots, LANES), jnp.int32)
    new_tile = jnp.full((slots, LANES), -1, jnp.int32)
    for s in range(slots):
        old_tile = jnp.where(sub8 == s, old_ref[0, s], old_tile)
        new_tile = jnp.where(lane8 == s, new_ref[0, s], new_tile)
    ids[0] = old_tile
    ids[1] = new_tile

    loads[3].wait()
    loads[4].wait()

    marks = (
        lax.broadcasted_iota(jnp.int32, (slots * group // 16, 16, LANES), 0) * 16
        + lax.broadcasted_iota(jnp.int32, (slots * group // 16, 16, LANES), 1)
    ).astype(jnp.float32).astype(jnp.bfloat16)
    offs_marks = (
        lax.broadcasted_iota(jnp.int32, (blk // 16, 16, LANES), 0) * 16
        + lax.broadcasted_iota(jnp.int32, (blk // 16, 16, LANES), 1)
    ).astype(jnp.float32).astype(jnp.bfloat16)
    lane = lax.broadcasted_iota(jnp.int32, (8, LANES), 1)
    sub = lax.broadcasted_iota(jnp.int32, (8, LANES), 0)
    in_group = sub + (lane // bag) * 8
    in_bag = lax.broadcasted_iota(jnp.int32, (bag, tile), 0)
    shift = blk.bit_length() - 1
    one = jnp.ones((), jnp.bfloat16)
    zero = jnp.zeros((), jnp.bfloat16)

    def spread(row, against):
        wide = jnp.broadcast_to(row, (16, LANES)).astype(jnp.bfloat16)
        hit = jnp.where(against == wide[None], one, zero)
        return hit.reshape(against.shape[0] * 16, LANES)

    def locate(first):
        bags = pl.ds(pl.multiple_of(first, tile), tile)
        wanted = jnp.where(in_bag < len_ref[:, bags], idx_ref[:, bags], -1)
        block = lax.shift_right_arithmetic(wanted, shift)
        off = wanted & (blk - 1)
        loc = jnp.full((bag, tile), -1, jnp.int32)
        for s in range(slots):
            loc = jnp.where(block == old_ref[0, s], off + s * blk, loc)
        turned = loc.astype(jnp.float32).T
        locs[...] = jnp.concatenate(
            [turned[i * half : (i + 1) * half] for i in range(pack)], axis=1
        ).astype(jnp.int32)

    def count_group(g):
        loc = locs[pl.ds(pl.multiple_of(g * 8, 8), 8), :]
        off = (loc & (blk - 1)).astype(jnp.float32)
        code = jnp.where(
            loc >= 0, lax.shift_right_arithmetic(loc, shift) * group + in_group, -1
        ).astype(jnp.float32)
        a = jnp.concatenate([spread(code[j : j + 1], marks) for j in range(8)], axis=1)
        b = jnp.concatenate([spread(off[j : j + 1], offs_marks) for j in range(8)], axis=1)
        n = lax.dot_general(a, b, (((1,), (1,)), ((), ())), preferred_element_type=jnp.float32)
        n = n.astype(jnp.bfloat16)
        at = pl.ds(pl.multiple_of(g * group, group), group)
        for s in range(slots):
            counts[at, s * blk : (s + 1) * blk] = n[s * group : (s + 1) * group]

    order = far_first(n_row)
    far = [q for q in order if q // 2]
    near = [q for q in order if not q // 2]

    def split_table():
        loads[2].wait()
        table = table_ref[...]
        high = table.astype(jnp.bfloat16)
        halves[:, :width] = high
        halves[:, width:] = (table - high.astype(jnp.float32)).astype(jnp.bfloat16)
        loads[5].start()
        loads[6].start()

    def pool_chunk(q, dest):
        def pool_tile(t):
            locate(dest * share + t * tile)

            def body(g, carry):
                count_group(g)
                return carry

            lax.fori_loop(0, tile // group, body, 0, unroll=UNROLL)
            if q == order[0] and isinstance(t, int):
                split_table()
            both = jnp.dot(counts[...], halves[...], preferred_element_type=jnp.float32)
            both = both[:, :width] + both[:, width:]
            for i in range(tile // 8):
                g, j = i // pack, i % pack
                at = pl.multiple_of(t * tile + j * half + g * 8, 8)
                part[q, pl.ds(at, 8)] = both[i * 8 : (i + 1) * 8]

        if share == tile:
            pool_tile(0)
        else:
            if q == order[0]:
                split_table()

            def step(t, carry):
                pool_tile(t)
                return carry

            lax.fori_loop(0, share // tile, step, 0)

    def to_row(q, src, dst, sems, rsems):
        copy = pltpu.make_async_remote_copy(
            src_ref=src, dst_ref=dst, send_sem=sems.at[q], recv_sem=rsems.at[q],
            device_id={"row": row_peer(r, q, n_row, 1)}, device_id_type=MESH,
        )
        copy.start()
        return copy

    def pick_blocks(q):
        theirs = new_tile if q == 0 else ids_in[q, 1]
        into = blocks_in if q == 0 else blocks_out
        codes = jnp.where(old_tile == theirs, lane8 * LANES + sub8, FAR)
        for m in range(move):
            first = least(codes)
            codes = jnp.where(codes > first, codes, FAR)
            into[q * move + m] = choose(first & (LANES - 1), [
                functools.partial(lambda s: table_ref[s * blk : (s + 1) * blk, :], s)
                for s in range(slots)
            ])

    def send_blocks(q):
        at = pl.ds(q * move, move)
        block_copies.append(to_row(q, blocks_out.at[at], blocks_in.at[at], blk_sem, blk_rsem))

    part_copies, id_copies, block_copies = [], {}, []
    pool_chunk(order[0], row_peer(r, order[0], n_row, 1))
    pl.semaphore_wait(barrier, n_row - 1 + n_col - 1)
    for q in order:
        id_copies[q] = to_row(q, ids, ids_in.at[q], ids_sem, ids_rsem)
    part_copies.append(to_row(order[0], part.at[order[0]], part_in.at[order[0]], part_sem, part_rsem))
    for q in far[1:]:
        pool_chunk(q, row_peer(r, q, n_row, 1))
        part_copies.append(to_row(q, part.at[q], part_in.at[q], part_sem, part_rsem))
    for q in near:
        pool_chunk(q, row_peer(r, q, n_row, 1))
        part_copies.append(to_row(q, part.at[q], part_in.at[q], part_sem, part_rsem))
    for q in order:
        id_copies[q].wait()
    for q in far:
        pick_blocks(q)
        send_blocks(q)
    pool_chunk(0, r)

    for copy in part_copies:
        copy.wait()
    acc = part[0]
    for q in range(1, n_row):
        acc = acc + part_in[q]
    total[...] = acc

    swaps = []
    for k in range(1, n_col):
        to = lax.rem(c + k, n_col)
        swap = pltpu.make_async_remote_copy(
            src_ref=total.at[pl.ds(pl.multiple_of(to * each, each), each)], dst_ref=stack.at[c + 1],
            send_sem=swap_sem.at[k], recv_sem=swap_rsem.at[k],
            device_id={"col": to}, device_id_type=MESH,
        )
        swap.start()
        swaps.append(swap)
    stack[0] = dense_ref[...].astype(jnp.float32)
    stack[c + 1] = total[pl.ds(pl.multiple_of(c * each, each), each), :]
    crossed_ref[...] = jnp.zeros_like(crossed_ref)
    lanes = lax.broadcasted_iota(jnp.int32, (each, LANES), 1)
    for q in near:
        pick_blocks(q)
        send_blocks(q)
    pick_blocks(0)

    where_in = jnp.zeros((slots, LANES), jnp.int32)
    for q in range(n_row):
        theirs = old_tile if q == 0 else ids_in[q, 0]
        hit = theirs == new_tile
        codes = jnp.where(hit, lane8, FAR)
        rank = jnp.zeros((slots, LANES), jnp.int32)
        left = codes
        for m in range(move - 1):
            first = least(left)
            rank = rank + jnp.where(codes > first, 1, 0)
            left = jnp.where(left > first, left, FAR)
        where_in = where_in + jnp.where(hit, q * move + rank, 0)
    sources = [everywhere(jnp.sum, jnp.where(lane8 == p, where_in, 0)) for p in range(slots)]
    for copy in block_copies:
        copy.wait()
    for p in range(slots):
        arranged[p] = choose(sources[p], [
            functools.partial(lambda at: blocks_in[at], at) for at in range(slots)
        ])
    loads[5].wait()
    loads[6].wait()
    for swap in swaps:
        swap.wait()

    count = n_col + 1
    pairs = count * (count - 1) // 2
    if pairs <= LANES:
        crossed = jnp.zeros((each, LANES), jnp.float32)
        k = 0
        for i in range(count):
            for j in range(i + 1, count):
                dot = jnp.sum(stack[i] * stack[j], axis=1, keepdims=True) * scale
                crossed = jnp.where(lanes == k, dot, crossed)
                k += 1
        crossed_ref[...] = crossed
    else:
        def rows(i, k):
            def cols(j, k):
                dot = jnp.sum(stack[i] * stack[j], axis=1, keepdims=True) * scale
                at = pl.ds(pl.multiple_of(k // LANES * LANES, LANES), LANES)
                crossed_ref[:, at] = jnp.where(lanes == k % LANES, dot, crossed_ref[:, at])
                return k + 1

            return lax.fori_loop(i + 1, count, cols, k)

        lax.fori_loop(0, count, rows, 0)
    crossed = crossed_ref[...].astype(jnp.bfloat16)[:, :pairs]
    hidden = jnp.dot(dense_ref[...], first_ref[:width, :], preferred_element_type=jnp.float32)
    hidden = hidden + jnp.dot(crossed, first_ref[width:, :], preferred_element_type=jnp.float32)
    hidden = jnp.maximum(hidden, 0.0).astype(jnp.bfloat16)
    hidden = jnp.dot(hidden, second_ref[...], preferred_element_type=jnp.float32)
    hidden = jnp.maximum(hidden, 0.0).astype(jnp.bfloat16).astype(jnp.float32)
    last = last_ref[...].astype(jnp.float32)
    acc = jnp.zeros((each, LANES), jnp.float32)
    for j in range(last.shape[0]):
        acc = acc + hidden[:, j * LANES : (j + 1) * LANES] * last[j : j + 1, :]
    logit = jnp.sum(acc, axis=1, keepdims=True)
    subs = lax.broadcasted_iota(jnp.int32, (each, LANES), 0)
    logits_ref[...] = jnp.sum(jnp.where(subs == lanes, logit, 0.0), axis=0, keepdims=True)[:, :each]


def write_out(logits_in, blocks, logits_hbm, out_hbm, sems):
    copies = [
        pltpu.make_async_copy(blocks, out_hbm, sems.at[0]),
        pltpu.make_async_copy(logits_in, logits_hbm, sems.at[1]),
    ]
    for copy in copies:
        copy.start()
    for copy in copies:
        copy.wait()


def step(n_row, n_col, old_blocks, new_blocks, table, wanted, lengths, dense, w_first, w_second, w_out):
    rows, width = table.shape
    slots = old_blocks.shape[1]
    blk = rows // slots
    bag, samples = wanted.shape
    share = samples // n_row
    each = share // n_col
    move = slots // n_row
    hbm = pl.BlockSpec(memory_space=pl.ANY)
    vmem = pl.BlockSpec(memory_space=pltpu.VMEM)
    dma = pltpu.SemaphoreType.DMA
    pairs = n_col * (n_col + 1) // 2
    logits, blocks = pl.pallas_call(
        functools.partial(kernel, n_row, n_col, width ** (-0.5)),
        out_shape=(
            pltpu.VMEM((1, each), jnp.float32),
            pltpu.VMEM((slots, blk, width), jnp.float32),
        ),
        in_specs=[hbm, hbm, hbm, hbm, hbm, vmem, hbm, hbm, vmem],
        out_specs=(vmem, vmem),
        scratch_shapes=[
            pltpu.SMEM(old_blocks.shape, jnp.int32),
            pltpu.SMEM(new_blocks.shape, jnp.int32),
            pltpu.VMEM((rows, width), jnp.float32),
            pltpu.VMEM(wanted.shape, jnp.int32),
            pltpu.VMEM(lengths.shape, jnp.int32),
            pltpu.VMEM(w_first.shape, jnp.bfloat16),
            pltpu.VMEM(w_second.shape, jnp.bfloat16),
            pltpu.VMEM((each, -(-pairs // LANES) * LANES), jnp.float32),
            pltpu.VMEM((2, slots, LANES), jnp.int32),
            pltpu.VMEM((n_row, 2, slots, LANES), jnp.int32),
            pltpu.VMEM((slots, blk, width), jnp.float32),
            pltpu.VMEM((slots, blk, width), jnp.float32),
            pltpu.VMEM((rows, 2 * width), jnp.bfloat16),
            pltpu.VMEM((bag, LANES), jnp.int32),
            pltpu.VMEM((LANES, rows), jnp.bfloat16),
            pltpu.VMEM((n_row, share, width), jnp.float32),
            pltpu.VMEM((n_row, share, width), jnp.float32),
            pltpu.VMEM((share, width), jnp.float32),
            pltpu.VMEM((n_col + 1, each, width), jnp.float32),
            dma((7,)),
            dma((n_row,)), dma((n_row,)),
            dma((n_row,)), dma((n_row,)),
            dma((n_row,)), dma((n_row,)),
            dma((n_col,)), dma((n_col,)),
        ],
        compiler_params=pltpu.CompilerParams(collective_id=0, has_side_effects=True),
    )(old_blocks, new_blocks, table, wanted, lengths, dense, w_first, w_second, w_out)
    return pl.pallas_call(
        write_out,
        out_shape=(
            jax.ShapeDtypeStruct((1, each), jnp.float32),
            jax.ShapeDtypeStruct((slots, blk, width), jnp.float32),
        ),
        in_specs=[hbm, hbm],
        out_specs=(hbm, hbm),
        scratch_shapes=[dma((2,))],
    )(
        pltpu.with_memory_space_constraint(logits, pltpu.VMEM),
        pltpu.with_memory_space_constraint(blocks, pltpu.VMEM),
    )


def shards(
    old_table, old_blocks, new_blocks, bag_row_index, bag_length, dense, w_first, w_second, w_out
):
    n_row, n_col = lax.axis_size("row"), lax.axis_size("col")
    logits, new_table = step(
        n_row, n_col, old_blocks, new_blocks, old_table[0], bag_row_index[:, 0, :].T, bag_length.T,
        dense, w_first, w_second, w_out.reshape(-1, LANES),
    )
    return logits.reshape(-1), new_table.reshape(old_table.shape)


def solution(mesh):
    in_specs = (
        P("col", "row", None),
        P("col", "row"),
        P("col", "row"),
        P(None, "col", None),
        P(None, "col"),
        P(("row", "col"), None),
        P(),
        P(),
        P(),
    )
    out_specs = (P(("row", "col")), P("col", "row", None))
    return jax.shard_map(shards, mesh=mesh, in_specs=in_specs, out_specs=out_specs, check_vma=False)
```

```python
import functools

import jax
import jax.numpy as jnp
from jax import lax
from jax.experimental import pallas as pl
from jax.experimental.pallas import tpu as pltpu
from jax.sharding import PartitionSpec as P

MESH = pl.DeviceIdType.MESH
LANES = 128
FAR = 1 << 20
UNROLL = 8


def row_peer(r, q, n, sign):
    chips = n // 2
    return lax.rem(r // 2 + (sign * (q // 2)) % chips, chips) * 2 + lax.rem(r % 2 + q % 2, 2)


def far_first(n):
    return sorted(range(1, n), key=lambda q: -(q // 2))


def everywhere(reduce, x):
    return reduce(reduce(x, axis=1, keepdims=True), axis=0, keepdims=True)


def least(x):
    return everywhere(jnp.min, x)


def choose(which, reads):
    first = reads[0]()
    rows, width = first.shape
    wide = jnp.broadcast_to(which, (8, width))
    picked = first.reshape(rows // 8, 8, width)
    for at, read in enumerate(reads[1:], 1):
        picked = jnp.where((wide == at)[None], read().reshape(rows // 8, 8, width), picked)
    return picked.reshape(rows, width)


def kernel(
    n_row, n_col, scale,
    old_hbm, new_hbm, table_hbm, idx_hbm, len_hbm, dense_ref, first_hbm, second_hbm, last_ref,
    logits_ref, arranged,
    old_ref, new_ref, table_ref, idx_ref, len_ref, first_ref, second_ref, crossed_ref,
    ids, ids_in, blocks_out, blocks_in, halves, locs, counts,
    part, part_in, total, stack,
    load_sem, ids_sem, ids_rsem, blk_sem, blk_rsem, part_sem, part_rsem, swap_sem, swap_rsem,
):
    r, c = lax.axis_index("row"), lax.axis_index("col")
    slots = old_ref.shape[1]
    blk = table_ref.shape[0] // slots
    width = table_ref.shape[1]
    move = slots // n_row
    bag, samples = idx_ref.shape
    share = samples // n_row
    each = share // n_col
    pack = LANES // bag
    group = 8 * pack
    tile = LANES
    half = tile // pack

    loads = [
        pltpu.make_async_copy(old_hbm, old_ref, load_sem.at[0]),
        pltpu.make_async_copy(new_hbm, new_ref, load_sem.at[1]),
        pltpu.make_async_copy(table_hbm, table_ref, load_sem.at[2]),
        pltpu.make_async_copy(idx_hbm, idx_ref, load_sem.at[3]),
        pltpu.make_async_copy(len_hbm, len_ref, load_sem.at[4]),
        pltpu.make_async_copy(first_hbm, first_ref, load_sem.at[5]),
        pltpu.make_async_copy(second_hbm, second_ref, load_sem.at[6]),
    ]
    for load in [loads[3], loads[4], loads[0], loads[1], loads[2]]:
        load.start()

    barrier = pltpu.get_barrier_semaphore()
    for k in range(1, n_col):
        pl.semaphore_signal(barrier, inc=1, device_id={"col": lax.rem(c + k, n_col)}, device_id_type=MESH)
    for q in range(1, n_row):
        pl.semaphore_signal(barrier, inc=1, device_id={"row": row_peer(r, q, n_row, 1)}, device_id_type=MESH)

    loads[0].wait()
    loads[1].wait()
    sub8 = lax.broadcasted_iota(jnp.int32, (slots, LANES), 0)
    lane8 = lax.broadcasted_iota(jnp.int32, (slots, LANES), 1)
    old_tile = jnp.zeros((slots, LANES), jnp.int32)
    new_tile = jnp.full((slots, LANES), -1, jnp.int32)
    for s in range(slots):
        old_tile = jnp.where(sub8 == s, old_ref[0, s], old_tile)
        new_tile = jnp.where(lane8 == s, new_ref[0, s], new_tile)
    ids[0] = old_tile
    ids[1] = new_tile

    loads[3].wait()
    loads[4].wait()

    marks = (
        lax.broadcasted_iota(jnp.int32, (slots * group // 16, 16, LANES), 0) * 16
        + lax.broadcasted_iota(jnp.int32, (slots * group // 16, 16, LANES), 1)
    ).astype(jnp.float32).astype(jnp.bfloat16)
    offs_marks = (
        lax.broadcasted_iota(jnp.int32, (blk // 16, 16, LANES), 0) * 16
        + lax.broadcasted_iota(jnp.int32, (blk // 16, 16, LANES), 1)
    ).astype(jnp.float32).astype(jnp.bfloat16)
    lane = lax.broadcasted_iota(jnp.int32, (8, LANES), 1)
    sub = lax.broadcasted_iota(jnp.int32, (8, LANES), 0)
    in_group = sub + (lane // bag) * 8
    in_bag = lax.broadcasted_iota(jnp.int32, (bag, tile), 0)
    shift = blk.bit_length() - 1
    one = jnp.ones((), jnp.bfloat16)
    zero = jnp.zeros((), jnp.bfloat16)

    def spread(row, against):
        wide = jnp.broadcast_to(row, (16, LANES)).astype(jnp.bfloat16)
        hit = jnp.where(against == wide[None], one, zero)
        return hit.reshape(against.shape[0] * 16, LANES)

    def locate(first):
        bags = pl.ds(pl.multiple_of(first, tile), tile)
        wanted = jnp.where(in_bag < len_ref[:, bags], idx_ref[:, bags], -1)
        block = lax.shift_right_arithmetic(wanted, shift)
        off = wanted & (blk - 1)
        loc = jnp.full((bag, tile), -1, jnp.int32)
        for s in range(slots):
            loc = jnp.where(block == old_ref[0, s], off + s * blk, loc)
        turned = loc.astype(jnp.float32).T
        locs[...] = jnp.concatenate(
            [turned[i * half : (i + 1) * half] for i in range(pack)], axis=1
        ).astype(jnp.int32)

    def count_group(g):
        loc = locs[pl.ds(pl.multiple_of(g * 8, 8), 8), :]
        off = (loc & (blk - 1)).astype(jnp.float32)
        code = jnp.where(
            loc >= 0, lax.shift_right_arithmetic(loc, shift) * group + in_group, -1
        ).astype(jnp.float32)
        a = jnp.concatenate([spread(code[j : j + 1], marks) for j in range(8)], axis=1)
        b = jnp.concatenate([spread(off[j : j + 1], offs_marks) for j in range(8)], axis=1)
        n = lax.dot_general(a, b, (((1,), (1,)), ((), ())), preferred_element_type=jnp.float32)
        n = n.astype(jnp.bfloat16)
        at = pl.ds(pl.multiple_of(g * group, group), group)
        for s in range(slots):
            counts[at, s * blk : (s + 1) * blk] = n[s * group : (s + 1) * group]

    order = far_first(n_row)
    far = [q for q in order if q // 2]
    near = [q for q in order if not q // 2]

    def split_table():
        loads[2].wait()
        table = table_ref[...]
        high = table.astype(jnp.bfloat16)
        halves[:, :width] = high
        halves[:, width:] = (table - high.astype(jnp.float32)).astype(jnp.bfloat16)
        loads[5].start()
        loads[6].start()

    def pool_chunk(q, dest):
        def pool_tile(t):
            locate(dest * share + t * tile)

            def body(g, carry):
                count_group(g)
                return carry

            lax.fori_loop(0, tile // group, body, 0, unroll=UNROLL)
            if q == order[0] and isinstance(t, int):
                split_table()
            both = jnp.dot(counts[...], halves[...], preferred_element_type=jnp.float32)
            both = both[:, :width] + both[:, width:]
            for i in range(tile // 8):
                g, j = i // pack, i % pack
                at = pl.multiple_of(t * tile + j * half + g * 8, 8)
                part[q, pl.ds(at, 8)] = both[i * 8 : (i + 1) * 8]

        if share == tile:
            pool_tile(0)
        else:
            if q == order[0]:
                split_table()

            def step(t, carry):
                pool_tile(t)
                return carry

            lax.fori_loop(0, share // tile, step, 0)

    def to_row(q, src, dst, sems, rsems):
        copy = pltpu.make_async_remote_copy(
            src_ref=src, dst_ref=dst, send_sem=sems.at[q], recv_sem=rsems.at[q],
            device_id={"row": row_peer(r, q, n_row, 1)}, device_id_type=MESH,
        )
        copy.start()
        return copy

    def pick_blocks(q):
        theirs = new_tile if q == 0 else ids_in[q, 1]
        into = blocks_in if q == 0 else blocks_out
        codes = jnp.where(old_tile == theirs, lane8 * LANES + sub8, FAR)
        for m in range(move):
            first = least(codes)
            codes = jnp.where(codes > first, codes, FAR)
            into[q * move + m] = choose(first & (LANES - 1), [
                functools.partial(lambda s: table_ref[s * blk : (s + 1) * blk, :], s)
                for s in range(slots)
            ])

    def send_blocks(q):
        at = pl.ds(q * move, move)
        block_copies.append(to_row(q, blocks_out.at[at], blocks_in.at[at], blk_sem, blk_rsem))

    part_copies, id_copies, block_copies = [], {}, []
    pool_chunk(order[0], row_peer(r, order[0], n_row, 1))
    pl.semaphore_wait(barrier, n_row - 1 + n_col - 1)
    for q in order:
        id_copies[q] = to_row(q, ids, ids_in.at[q], ids_sem, ids_rsem)
    part_copies.append(to_row(order[0], part.at[order[0]], part_in.at[order[0]], part_sem, part_rsem))
    for q in far[1:]:
        pool_chunk(q, row_peer(r, q, n_row, 1))
        part_copies.append(to_row(q, part.at[q], part_in.at[q], part_sem, part_rsem))
    for q in near:
        pool_chunk(q, row_peer(r, q, n_row, 1))
        part_copies.append(to_row(q, part.at[q], part_in.at[q], part_sem, part_rsem))
    for q in order:
        id_copies[q].wait()
    for q in far:
        pick_blocks(q)
        send_blocks(q)
    pool_chunk(0, r)

    for copy in part_copies:
        copy.wait()
    acc = part[0]
    for q in range(1, n_row):
        acc = acc + part_in[q]
    total[...] = acc

    swaps = []
    for k in range(1, n_col):
        to = lax.rem(c + k, n_col)
        swap = pltpu.make_async_remote_copy(
            src_ref=total.at[pl.ds(pl.multiple_of(to * each, each), each)], dst_ref=stack.at[c + 1],
            send_sem=swap_sem.at[k], recv_sem=swap_rsem.at[k],
            device_id={"col": to}, device_id_type=MESH,
        )
        swap.start()
        swaps.append(swap)
    stack[0] = dense_ref[...].astype(jnp.float32)
    stack[c + 1] = total[pl.ds(pl.multiple_of(c * each, each), each), :]
    crossed_ref[...] = jnp.zeros_like(crossed_ref)
    lanes = lax.broadcasted_iota(jnp.int32, (each, LANES), 1)
    for q in near:
        pick_blocks(q)
        send_blocks(q)
    pick_blocks(0)

    where_in = jnp.zeros((slots, LANES), jnp.int32)
    for q in range(n_row):
        theirs = old_tile if q == 0 else ids_in[q, 0]
        hit = theirs == new_tile
        codes = jnp.where(hit, lane8, FAR)
        rank = jnp.zeros((slots, LANES), jnp.int32)
        left = codes
        for m in range(move - 1):
            first = least(left)
            rank = rank + jnp.where(codes > first, 1, 0)
            left = jnp.where(left > first, left, FAR)
        where_in = where_in + jnp.where(hit, q * move + rank, 0)
    sources = [everywhere(jnp.sum, jnp.where(lane8 == p, where_in, 0)) for p in range(slots)]
    loads[5].wait()
    loads[6].wait()
    for swap in swaps:
        swap.wait()

    count = n_col + 1
    pairs = count * (count - 1) // 2
    if pairs <= LANES:
        crossed = jnp.zeros((each, LANES), jnp.float32)
        k = 0
        for i in range(count):
            for j in range(i + 1, count):
                dot = jnp.sum(stack[i] * stack[j], axis=1, keepdims=True) * scale
                crossed = jnp.where(lanes == k, dot, crossed)
                k += 1
        crossed_ref[...] = crossed
    else:
        def rows(i, k):
            def cols(j, k):
                dot = jnp.sum(stack[i] * stack[j], axis=1, keepdims=True) * scale
                at = pl.ds(pl.multiple_of(k // LANES * LANES, LANES), LANES)
                crossed_ref[:, at] = jnp.where(lanes == k % LANES, dot, crossed_ref[:, at])
                return k + 1

            return lax.fori_loop(i + 1, count, cols, k)

        lax.fori_loop(0, count, rows, 0)
    crossed = crossed_ref[...].astype(jnp.bfloat16)[:, :pairs]
    hidden = jnp.dot(dense_ref[...], first_ref[:width, :], preferred_element_type=jnp.float32)
    hidden = hidden + jnp.dot(crossed, first_ref[width:, :], preferred_element_type=jnp.float32)
    hidden = jnp.maximum(hidden, 0.0).astype(jnp.bfloat16)
    hidden = jnp.dot(hidden, second_ref[...], preferred_element_type=jnp.float32)
    hidden = jnp.maximum(hidden, 0.0).astype(jnp.bfloat16).astype(jnp.float32)
    last = last_ref[...].astype(jnp.float32)
    acc = jnp.zeros((each, LANES), jnp.float32)
    for j in range(last.shape[0]):
        acc = acc + hidden[:, j * LANES : (j + 1) * LANES] * last[j : j + 1, :]
    logit = jnp.sum(acc, axis=1, keepdims=True)
    subs = lax.broadcasted_iota(jnp.int32, (each, LANES), 0)
    logits_ref[...] = jnp.sum(jnp.where(subs == lanes, logit, 0.0), axis=0, keepdims=True)[:, :each]

    for copy in block_copies:
        copy.wait()
    for p in range(slots):
        arranged[p] = choose(sources[p], [
            functools.partial(lambda at: blocks_in[at], at) for at in range(slots)
        ])


def write_out(logits_in, blocks, logits_hbm, out_hbm, sems):
    copies = [
        pltpu.make_async_copy(blocks, out_hbm, sems.at[0]),
        pltpu.make_async_copy(logits_in, logits_hbm, sems.at[1]),
    ]
    for copy in copies:
        copy.start()
    for copy in copies:
        copy.wait()


def step(n_row, n_col, old_blocks, new_blocks, table, wanted, lengths, dense, w_first, w_second, w_out):
    rows, width = table.shape
    slots = old_blocks.shape[1]
    blk = rows // slots
    bag, samples = wanted.shape
    share = samples // n_row
    each = share // n_col
    move = slots // n_row
    hbm = pl.BlockSpec(memory_space=pl.ANY)
    vmem = pl.BlockSpec(memory_space=pltpu.VMEM)
    dma = pltpu.SemaphoreType.DMA
    pairs = n_col * (n_col + 1) // 2
    logits, blocks = pl.pallas_call(
        functools.partial(kernel, n_row, n_col, width ** (-0.5)),
        out_shape=(
            pltpu.VMEM((1, each), jnp.float32),
            pltpu.VMEM((slots, blk, width), jnp.float32),
        ),
        in_specs=[hbm, hbm, hbm, hbm, hbm, vmem, hbm, hbm, vmem],
        out_specs=(vmem, vmem),
        scratch_shapes=[
            pltpu.SMEM(old_blocks.shape, jnp.int32),
            pltpu.SMEM(new_blocks.shape, jnp.int32),
            pltpu.VMEM((rows, width), jnp.float32),
            pltpu.VMEM(wanted.shape, jnp.int32),
            pltpu.VMEM(lengths.shape, jnp.int32),
            pltpu.VMEM(w_first.shape, jnp.bfloat16),
            pltpu.VMEM(w_second.shape, jnp.bfloat16),
            pltpu.VMEM((each, -(-pairs // LANES) * LANES), jnp.float32),
            pltpu.VMEM((2, slots, LANES), jnp.int32),
            pltpu.VMEM((n_row, 2, slots, LANES), jnp.int32),
            pltpu.VMEM((slots, blk, width), jnp.float32),
            pltpu.VMEM((slots, blk, width), jnp.float32),
            pltpu.VMEM((rows, 2 * width), jnp.bfloat16),
            pltpu.VMEM((bag, LANES), jnp.int32),
            pltpu.VMEM((LANES, rows), jnp.bfloat16),
            pltpu.VMEM((n_row, share, width), jnp.float32),
            pltpu.VMEM((n_row, share, width), jnp.float32),
            pltpu.VMEM((share, width), jnp.float32),
            pltpu.VMEM((n_col + 1, each, width), jnp.float32),
            dma((7,)),
            dma((n_row,)), dma((n_row,)),
            dma((n_row,)), dma((n_row,)),
            dma((n_row,)), dma((n_row,)),
            dma((n_col,)), dma((n_col,)),
        ],
        compiler_params=pltpu.CompilerParams(collective_id=0, has_side_effects=True),
    )(old_blocks, new_blocks, table, wanted, lengths, dense, w_first, w_second, w_out)
    return pl.pallas_call(
        write_out,
        out_shape=(
            jax.ShapeDtypeStruct((1, each), jnp.float32),
            jax.ShapeDtypeStruct((slots, blk, width), jnp.float32),
        ),
        in_specs=[hbm, hbm],
        out_specs=(hbm, hbm),
        scratch_shapes=[dma((2,))],
    )(
        pltpu.with_memory_space_constraint(logits, pltpu.VMEM),
        pltpu.with_memory_space_constraint(blocks, pltpu.VMEM),
    )


def shards(
    old_table, old_blocks, new_blocks, bag_row_index, bag_length, dense, w_first, w_second, w_out
):
    n_row, n_col = lax.axis_size("row"), lax.axis_size("col")
    logits, new_table = step(
        n_row, n_col, old_blocks, new_blocks, old_table[0], bag_row_index[:, 0, :].T, bag_length.T,
        dense, w_first, w_second, w_out.reshape(-1, LANES),
    )
    return logits.reshape(-1), new_table.reshape(old_table.shape)


def solution(mesh):
    in_specs = (
        P("col", "row", None),
        P("col", "row"),
        P("col", "row"),
        P(None, "col", None),
        P(None, "col"),
        P(("row", "col"), None),
        P(),
        P(),
        P(),
    )
    out_specs = (P(("row", "col")), P("col", "row", None))
    return jax.shard_map(shards, mesh=mesh, in_specs=in_specs, out_specs=out_specs, check_vma=False)
```
